32 devices in a mesh: shard: 2 (over x), ctx: 4 (over z), tp: 4 (over y, core).
Axes of the slice: x: 2, y: 2, z: 4, core: 2. Of those that a mesh axis runs over, the one named last changes fastest.
Arguments:
- tokens: bfloat16 [8, 2048, 768], P('shard', 'ctx'), may hold values from -6 to 6
- segments: int32 [8, 2048], P('shard', 'ctx'), may hold values from 0 to 3, as said below
- timesteps: int32 [8], P('shard'), may hold values from 0 to 1999
- w_time1: bfloat16 [128, 768], P('shard'), may hold values from -0.75 to 0.75
- w_time2: bfloat16 [768, 768], P('shard'), may hold values from -0.21875 to 0.21875
- w_qkv: bfloat16 [768, 3, 768], P('shard', None, 'tp'), may hold values from -0.21875 to 0.21875
- w_out: bfloat16 [768, 768], P(('tp', 'shard')), may hold values from -2.5 to 2.5
- w_in: bfloat16 [768, 3072], P('shard', 'tp'), may hold values from -0.21875 to 0.21875
- w_down: bfloat16 [3072, 768], P(('tp', 'shard')), may hold values from -0.15625 to 0.15625
- norm_gains: bfloat16 [768, 2], P('shard'), may hold values from 0.3984375 to 1.59375
- norm_shifts: bfloat16 [768, 2], P('shard'), may hold values from -1.5 to 1.5
- cotangent: bfloat16 [8, 2048, 768], P('shard', 'ctx'), may hold values from -6 to 6
Outputs:
- output: bfloat16 [8, 2048, 768], P('shard', 'ctx')
- grad_tokens: float32 [8, 2048, 768], P('shard', 'ctx')
- grad_time1: float32 [128, 768], P('shard')
- grad_time2: float32 [768, 768], P('shard')
- grad_qkv: float32 [768, 3, 768], P('shard', None, 'tp')
- grad_out: float32 [768, 768], P(('tp', 'shard'))
- grad_in: float32 [768, 3072], P('shard', 'tp')
- grad_down: float32 [3072, 768], P(('tp', 'shard'))
- grad_gains: float32 [768, 2], P('shard')
- grad_shifts: float32 [768, 2], P('shard')
The draws below stay inside these ranges and needn't reach their ends.
Inputs may be any that keep to these rules, and one draw needn't show every extreme that they name: `segments`: along each sequence the numbers never fall; a sequence holds two to four documents, each one run of 200 or more positions.
All inputs are finite; a program needn't handle non-finite values.
Results may differ from the reference program's by a relative error of at most 0.022.
Values may be sent and summed in bfloat16 or wider, within the bound.
A program may use at most 192 MiB of HBM per device.

```python
import math
import jax
import jax.numpy as jnp
from jax import lax

D = 768
HEADS = 12
FF = 3072
TIME_DIM = 128
HEAD_DIM = 64
LEN = 2048
DOC_MIN = 200
SEQS = 8


def draw_segments(key, part):
    base = jax.random.fold_in(key, 11)
    counts = jax.random.randint(jax.random.fold_in(base, 1), (SEQS,), 2, 5)
    order = jnp.arange(SEQS)
    counts = jnp.where(order == 0, 4, jnp.where(order == 1, 2, counts))
    room = LEN - counts * DOC_MIN
    raw = jax.random.randint(jax.random.fold_in(base, 2), (SEQS, 3), 0, 1 << 30)
    offsets = raw % (room[:, None] + 1)
    slot = jnp.arange(1, 4)
    valid = slot[None, :] < counts[:, None]
    offsets = jnp.sort(jnp.where(valid, offsets, LEN), axis=1)
    cuts = jnp.where(valid, offsets + slot[None, :] * DOC_MIN, LEN)
    positions = jnp.arange(LEN)
    return jnp.sum((positions[None, :, None] >= cuts[:, None, :]).astype(jnp.int32), axis=2)


def with_ends(entries, stream_key, least, top_value):
    index_at = [jax.random.randint(jax.random.fold_in(stream_key, axis), (), 0, length) for axis, length in enumerate(entries.shape)]
    longest = entries.shape.index(max(entries.shape))
    next_to = index_at[:longest] + [(index_at[longest] + 1) % entries.shape[longest]] + index_at[longest + 1:]
    return entries.at[tuple(index_at)].set(least).at[tuple(next_to)].set(top_value)


def shard_levels(own_key, extent, pieces, low, top_value):
    factor_of = 1.0
    for dim, shards_of in pieces:
        steps = jax.random.uniform(jax.random.fold_in(jax.random.fold_in(own_key, 6), dim), (shards_of,), jnp.float32, low / len(pieces), top_value / len(pieces))
        factor_of = factor_of * jnp.repeat(jnp.exp(steps), extent[dim] // shards_of).reshape((-1,) + (1,) * (len(extent) - 1 - dim))
    return factor_of


def noise(key, dims, scale, bound, split=(), kind=jnp.bfloat16):
    factor_of = shard_levels(key, dims, split, -0.22, 0.18) if split else 1.0
    entries = jax.random.normal(key, dims, jnp.float32) * scale * factor_of
    return jnp.minimum(jnp.maximum(entries, -bound), bound).astype(kind)


def setup_inputs(seed: int = 0) -> dict:
    seeds = jax.random.split(jax.random.key(seed), 13)
    return {
        "tokens": noise(seeds[0], (SEQS, LEN, D), 1.0, 6.0, ((0, 2), (1, 4))),
        "segments": draw_segments(jax.random.fold_in(seeds[12], 71), 0),
        "timesteps": with_ends(jax.random.randint(seeds[2], (SEQS,), 0, 2000), jax.random.fold_in(seeds[2], 1), 0, 1999).astype(jnp.int32),
        "w_time1": noise(seeds[3], (TIME_DIM, D), (TIME_DIM // 2) ** -0.5, 0.75, ((0, 2),)),
        "w_time2": noise(seeds[4], (D, D), D ** -0.5, 0.21875, ((0, 2),)),
        "w_qkv": noise(seeds[5], (D, 3, D), D ** -0.5, 0.21875, ((0, 2), (2, 4))),
        "w_out": noise(seeds[6], (D, D), (D * 16 // LEN) ** -0.5, 2.5, ((0, 8),)),
        "w_in": noise(seeds[7], (D, FF), D ** -0.5, 0.21875, ((0, 2), (1, 4))),
        "w_down": noise(seeds[8], (FF, D), (FF // 2) ** -0.5, 0.15625, ((0, 8),)),
        "norm_gains": jnp.clip(1.0 + 0.12 * jax.random.normal(seeds[9], (D, 2), jnp.float32), 0.3984375, 1.59375).astype(jnp.bfloat16),
        "norm_shifts": noise(seeds[10], (D, 2), 0.3, 1.5, ((0, 2),)),
        "cotangent": noise(seeds[11], (SEQS, LEN, D), 1.0, 6.0, ((0, 2), (1, 4))),
    }


@jax.custom_vjp
def low(v):
    return lax.optimization_barrier(v.astype(jnp.bfloat16)).astype(jnp.float32)

@jax.custom_vjp
def low_back(v):
    return v

def low_keep(v):
    return (low(v), None)

def low_pass(kept, grad):
    return (grad,)

def back_keep(v):
    return (v, None)

def back_low(kept, grad):
    return (low(grad),)
low.defvjp(low_keep, low_pass)
low_back.defvjp(back_keep, back_low)
NORM_EPS = 1e-05
MASKED = -1000000000.0

def time_features(steps_in, width):
    half = width // 2
    ratios = jnp.exp(-math.log(10000.0) * jnp.arange(half, dtype=jnp.float32) / half)
    angles = steps_in.astype(jnp.float32)[:, None] * ratios[None, :]
    return jnp.concatenate([jnp.cos(angles), jnp.sin(angles)], axis=1)

def silu_fn(value):
    return value / (1.0 + jnp.exp(-value))

def gelu_fn(value):
    return 0.5 * value * (1.0 + lax.erf(value * (1.0 / math.sqrt(2.0))))

def product(left, right):
    return jnp.dot(left, right, precision=lax.Precision.HIGHEST)

def layer_norm(rows, gain, shift):
    mean = lax.optimization_barrier(jnp.mean(rows, axis=-1, keepdims=True))
    centred = rows - mean
    inverse = lax.rsqrt(lax.optimization_barrier(jnp.mean(centred * centred, axis=-1, keepdims=True)) + NORM_EPS)
    return centred * inverse * gain + shift

def one_sequence(pack, params):
    seq_tokens, segment, feats = pack
    w_time1, w_time2, w_qkv, w_out, w_in, w_down, gains, shifts = params
    time_pre = low_back(product(feats[None, :], w_time1))
    time_hidden = low(silu_fn(time_pre))
    time_embed = low_back(product(time_hidden, w_time2))
    mixed = seq_tokens + time_embed
    joint = product(low(mixed), w_qkv.reshape(D, 3 * D))
    queries = low_back(low(joint[:, :D])).reshape(LEN, HEADS, HEAD_DIM)
    keys = low_back(low(joint[:, D:2 * D])).reshape(LEN, HEADS, HEAD_DIM)
    values = low_back(low(joint[:, 2 * D:])).reshape(LEN, HEADS, HEAD_DIM)
    scores = jnp.einsum('qhd,khd->hqk', queries, keys, precision=lax.Precision.HIGHEST) * HEAD_DIM ** (-0.5)
    scores = low_back(scores)
    same = segment[:, None] == segment[None, :]
    scores = jnp.where(same[None, :, :], scores, MASKED)
    scores = scores - lax.optimization_barrier(jnp.max(scores, axis=-1, keepdims=True))
    expd = jnp.exp(scores)
    probs = expd / lax.optimization_barrier(jnp.sum(expd, axis=-1, keepdims=True))
    weighted = jnp.einsum('hqk,khd->qhd', low(probs), values, precision=lax.Precision.HIGHEST)
    attended = low_back(low(weighted.reshape(LEN, D)))
    branch = low_back(product(attended, w_out))
    first = layer_norm(mixed + branch, gains[:, 0], shifts[:, 0])
    inner = low_back(product(low(first), w_in))
    activated = low(gelu_fn(inner))
    second = first + low_back(product(activated, w_down))
    return layer_norm(second, gains[:, 1], shifts[:, 1])

def reference(tokens, segments, timesteps, w_time1, w_time2, w_qkv, w_out, w_in, w_down, norm_gains, norm_shifts, cotangent):
    feats_all = low(time_features(timesteps, TIME_DIM))
    params = (w_time1.astype(jnp.float32), w_time2.astype(jnp.float32), w_qkv.astype(jnp.float32), w_out.astype(jnp.float32), w_in.astype(jnp.float32), w_down.astype(jnp.float32), norm_gains.astype(jnp.float32), norm_shifts.astype(jnp.float32))

    def forward(inputs, weights):

        def each(pack):
            return one_sequence(pack, weights)
        return lax.map(jax.checkpoint(each), (inputs, segments, feats_all))
    result, pullback = jax.vjp(forward, tokens.astype(jnp.float32), params)
    grad_tokens, grads = pullback(cotangent.astype(jnp.float32))
    return (result.astype(jnp.bfloat16), grad_tokens, grads[0], grads[1], grads[2], grads[3], grads[4], grads[5], grads[6], grads[7])
```

```python
import functools
import math

import jax
import jax.numpy as jnp
from jax import lax
from jax.experimental import pallas as pl
from jax.experimental.pallas import tpu as pltpu
from jax.sharding import PartitionSpec as P

HEAD_DIM = 64
NORM_EPS = 1e-05
BIG = 1e30
BF = jnp.bfloat16
F32 = jnp.float32
MESH = pl.DeviceIdType.MESH


def time_features(steps_in, width):
    half = width // 2
    ratios = jnp.exp(-math.log(10000.0) * jnp.arange(half, dtype=F32) / half)
    angles = steps_in.astype(F32)[:, None] * ratios[None, :]
    return jnp.concatenate([jnp.cos(angles), jnp.sin(angles)], axis=1)


def silu_fn(value):
    return value / (1.0 + jnp.exp(-value))


def gelu_pair(v):
    half = 0.5 * (1.0 + lax.erf(v * (1.0 / math.sqrt(2.0))))
    bell = jnp.exp(-0.5 * v * v) * (1.0 / math.sqrt(2.0 * math.pi))
    return v * half, half + v * bell


def contract(left, right, ldim, rdim):
    return lax.dot_general(left, right, (((ldim,), (rdim,)), ((), ())), preferred_element_type=F32)


def dot(a, b):
    return contract(a, b, 1, 0)


def send(src, dst, send_sem, recv_sem, **where):
    return pltpu.make_async_remote_copy(
        src_ref=src, dst_ref=dst, send_sem=send_sem, recv_sem=recv_sem,
        device_id=where, device_id_type=MESH,
    )


def meet(peers):
    barrier = pltpu.get_barrier_semaphore()
    for where in peers:
        pl.semaphore_signal(barrier, inc=1, device_id=where, device_id_type=MESH)
    pl.semaphore_wait(barrier, len(peers))


def attend_kernel(heads, bk, lo_ref, hi_ref, qt_ref, kv_ref, aq_ref, ak_ref, ot_ref, lse_ref, ka, vat):
    i = pl.program_id(0)
    hd = qt_ref.shape[0] // heads
    parts, _, piece = ot_ref.shape
    each = range(heads)

    @pl.when(i == 0)
    def _():
        for h in each:
            ka[h] = jnp.concatenate([kv_ref[h * hd : (h + 1) * hd], ak_ref[...]], axis=0).T
            vat[h] = jnp.concatenate([kv_ref[(heads + h) * hd : (heads + h + 1) * hd], ak_ref[:16, :]], axis=0)

    bq = qt_ref.shape[1]
    qa = [jnp.concatenate([qt_ref[h * hd : (h + 1) * hd], aq_ref[...]], axis=0) for h in each]

    def step(j, carry):
        off = pl.multiple_of(j * bk, bk)
        s = [dot(ka[h, pl.ds(off, bk), :], qa[h]) for h in each]
        out = []
        for h in each:
            m, acc = carry[h]
            mn = jnp.maximum(m, jnp.max(s[h], axis=0, keepdims=True))
            p = jnp.exp(s[h] - mn).astype(BF)
            out.append((mn, acc * jnp.exp(m - mn) + dot(vat[h, :, pl.ds(off, bk)], p)))
        return tuple(out)

    m0 = jnp.full((1, bq), -BIG * 2, F32)
    a0 = jnp.zeros((hd + 16, bq), F32)
    done = lax.fori_loop(lo_ref[i], hi_ref[i], step, ((m0, a0),) * heads)
    for h in each:
        m, acc = done[h]
        total = acc[hd + 4 : hd + 5, :]
        out = (acc[:hd, :] / total).astype(BF)
        for t in range(parts):
            ot_ref[t, h * hd : (h + 1) * hd, :] = out[:, t * piece : (t + 1) * piece]
        lse_ref[h] = m + jnp.log(total)


def attend(joint_t, aq, ak, lo, hi, heads, hd, parts, bq, bk):
    n = joint_t.shape[1]
    w = heads * hd
    piece = bq // parts
    return pl.pallas_call(
        functools.partial(attend_kernel, heads, bk),
        out_shape=(
            jax.ShapeDtypeStruct((parts, w, n // parts), BF),
            jax.ShapeDtypeStruct((heads, 1, n), F32),
        ),
        grid_spec=pltpu.PrefetchScalarGridSpec(
            num_scalar_prefetch=2,
            grid=(n // bq,),
            in_specs=[
                pl.BlockSpec((w, bq), lambda i, *_: (0, i)),
                pl.BlockSpec((2 * w, n), lambda i, *_: (0, 0)),
                pl.BlockSpec((64, bq), lambda i, *_: (0, i)),
                pl.BlockSpec((64, n), lambda i, *_: (0, 0)),
            ],
            out_specs=[
                pl.BlockSpec((parts, w, piece), lambda i, *_: (0, 0, i)),
                pl.BlockSpec((heads, 1, bq), lambda i, *_: (0, 0, i)),
            ],
            scratch_shapes=[
                pltpu.VMEM((heads, n, hd + 64), BF),
                pltpu.VMEM((heads, hd + 16, n), BF),
            ],
        ),
        name="attend",
        cost_estimate=pl.CostEstimate(
            flops=4 * heads * n * n * hd, bytes_accessed=8 * heads * n * hd, transcendentals=heads * n * n
        ),
    )(lo, hi, joint_t[:w], joint_t[w:], aq, ak)


def split3(v):
    a = v.astype(BF)
    r = v - a.astype(F32)
    b = r.astype(BF)
    c = (r - b.astype(F32)).astype(BF)
    return a, b, c


def attend_back_kernel(
    heads, bk, scale, lo_ref, hi_ref, qt_ref, kv_ref, aq_ref, ak_ref, ot_ref, gt_ref, lse_ref,
    dq_ref, dkv_ref, ka, va, acc,
):
    i = pl.program_id(0)
    w, bq = qt_ref.shape
    parts = ot_ref.shape[0]
    hd = w // heads
    each = range(heads)

    @pl.when(i == 0)
    def _():
        for h in each:
            ka[h] = jnp.concatenate([kv_ref[h * hd : (h + 1) * hd], ak_ref[...]], axis=0).T
            va[h] = jnp.concatenate([kv_ref[(heads + h) * hd : (heads + h + 1) * hd], ak_ref[...]], axis=0).T
        acc[...] = jnp.zeros_like(acc)

    row = lax.broadcasted_iota(jnp.int32, (64, bq), 0)

    def rows3(v):
        a, b, c = split3(v)
        return (
            jnp.where(row == 4, a.astype(F32), 0.0)
            + jnp.where(row == 5, b.astype(F32), 0.0)
            + jnp.where(row == 6, c.astype(F32), 0.0)
        )

    qa, ga, right = [], [], []
    for h in each:
        part = slice(h * hd, (h + 1) * hd)
        qt = qt_ref[part]
        gt = jnp.concatenate([gt_ref[t, part, :] for t in range(parts)], axis=1)
        ot = jnp.concatenate([ot_ref[t, part, :] for t in range(parts)], axis=1)
        delta = jnp.sum(gt.astype(F32) * ot.astype(F32), axis=0, keepdims=True)
        qa.append(jnp.concatenate([qt, (aq_ref[...].astype(F32) + rows3(-lse_ref[h])).astype(BF)], axis=0))
        ga.append(jnp.concatenate([gt, rows3(-delta).astype(BF)], axis=0))
        zero = jnp.zeros_like(qt)
        right.append(
            jnp.concatenate(
                [jnp.concatenate([qt, zero], axis=0).T, jnp.concatenate([zero, gt], axis=0).T], axis=0
            )
        )

    def step(j, dq):
        off = pl.multiple_of(j * bk, bk)
        s = [dot(ka[h, pl.ds(off, bk), :], qa[h]) for h in each]
        g = [dot(va[h, pl.ds(off, bk), :], ga[h]) for h in each]
        out = []
        for h in each:
            p = jnp.exp(s[h])
            ds = (p * g[h]).astype(BF)
            acc[h, pl.ds(off, bk), :] += dot(jnp.concatenate([ds, p.astype(BF)], axis=1), right[h])
            out.append(dq[h] + dot(kv_ref[h * hd : (h + 1) * hd, pl.ds(off, bk)], ds))
        return tuple(out)

    dq = lax.fori_loop(lo_ref[i], hi_ref[i], step, (jnp.zeros((hd, bq), F32),) * heads)
    for h in each:
        dq_ref[h * hd : (h + 1) * hd] = (dq[h] * scale).astype(BF)

    @pl.when(i == pl.num_programs(0) - 1)
    def _():
        for h in each:
            full = acc[h].T
            dkv_ref[h * hd : (h + 1) * hd] = full[:hd].astype(BF)
            dkv_ref[(heads + h) * hd : (heads + h + 1) * hd] = full[hd:].astype(BF)


def attend_back(joint_t, aq, ak, ot, got, lse, lo, hi, heads, hd, parts, bq, bk):
    n = joint_t.shape[1]
    w = heads * hd
    piece = bq // parts
    return pl.pallas_call(
        functools.partial(attend_back_kernel, heads, bk, hd ** -0.5),
        out_shape=(jax.ShapeDtypeStruct((w, n), BF), jax.ShapeDtypeStruct((2 * w, n), BF)),
        grid_spec=pltpu.PrefetchScalarGridSpec(
            num_scalar_prefetch=2,
            grid=(n // bq,),
            in_specs=[
                pl.BlockSpec((w, bq), lambda i, *_: (0, i)),
                pl.BlockSpec((2 * w, n), lambda i, *_: (0, 0)),
                pl.BlockSpec((64, bq), lambda i, *_: (0, i)),
                pl.BlockSpec((64, n), lambda i, *_: (0, 0)),
                pl.BlockSpec((parts, w, piece), lambda i, *_: (0, 0, i)),
                pl.BlockSpec((parts, w, piece), lambda i, *_: (0, 0, i)),
                pl.BlockSpec((heads, 1, bq), lambda i, *_: (0, 0, i)),
            ],
            out_specs=[
                pl.BlockSpec((w, bq), lambda i, *_: (0, i)),
                pl.BlockSpec((2 * w, n), lambda i, *_: (0, 0)),
            ],
            scratch_shapes=[
                pltpu.VMEM((heads, n, hd + 64), BF),
                pltpu.VMEM((heads, n, hd + 64), BF),
                pltpu.VMEM((heads, n, 2 * hd), F32),
            ],
        ),
        name="attend_back",
        cost_estimate=pl.CostEstimate(
            flops=10 * heads * n * n * hd, bytes_accessed=16 * heads * n * hd, transcendentals=heads * n * n
        ),
    )(lo, hi, joint_t[:w], joint_t[w:], aq, ak, ot, got, lse)


def mask_rows(seg):
    n = seg.shape[0]
    one = seg[None, :] == jnp.arange(4, dtype=jnp.int32)[:, None]
    aq = jnp.concatenate([jnp.where(one, 0.0, -BIG).astype(BF), jnp.zeros((60, n), BF)], axis=0)
    ak = jnp.concatenate([one.astype(BF), jnp.ones((3, n), BF), jnp.zeros((57, n), BF)], axis=0)
    return aq, ak


def key_ranges(seg, bq, bk):
    first = seg[::bq]
    last = seg[bq - 1 :: bq]
    lo = jnp.sum(seg[None, :] < first[:, None], axis=1) // bk
    hi = (jnp.sum(seg[None, :] <= last[:, None], axis=1) + bk - 1) // bk
    return lo.astype(jnp.int32), hi.astype(jnp.int32)


def spread_kernel(extras, src, *refs):
    ins, dst, outs = refs[:extras], refs[extras], refs[extras + 1 : 2 * extras + 1]
    loc, zs, zr, ys, yr, cs, cr, es, er = refs[2 * extras + 1 :]
    z, q = lax.axis_index("ctx"), lax.axis_index("tp")
    count = lax.axis_size("ctx")
    wide = extras > 0
    rows = dst.shape[1] // lax.axis_size("tp")
    mine = pl.ds(pl.multiple_of(q * rows, rows), rows)
    far = q ^ 2
    far_rows = pl.ds(pl.multiple_of(far * rows, rows), rows)
    meet([{"ctx": lax.rem(z + d, count)} for d in range(1, count)] + [{"tp": q ^ 1}, {"tp": q ^ 2}])

    def hop(d):
        to = lax.rem(z + d, count)
        block = src.at[to, mine] if wide else src.at[to]
        return send(block, dst.at[z, mine], zs.at[d], zr.at[d], ctx=to)

    def part(ref, out, c):
        return ref.at[c] if ref.shape == out.shape else ref.at[c, mine]

    def hop_extra(e, d):
        to = lax.rem(z + d, count)
        return send(part(ins[e], outs[e], to), outs[e].at[z], es.at[e, d], er.at[e, d], ctx=to)

    for d in range(1, count):
        hop(d).start()
    if wide:
        keep = [pltpu.make_async_copy(src.at[z], dst.at[z], loc.at[0])]
        for e in range(extras):
            keep.append(pltpu.make_async_copy(part(ins[e], outs[e], z), outs[e].at[z], loc.at[e + 1]))
        for copy in keep:
            copy.start()
        for e in range(extras):
            for d in range(1, count):
                hop_extra(e, d).start()
        order = list(range(1, count))
    else:
        own = pltpu.make_async_copy(src.at[z], dst.at[z, mine], loc.at[0])
        own.start()
        own.wait()
        keep = []
        order = list(range(count))

    def across(d):
        at = dst.at[lax.rem(z + count - d, count), mine]
        return send(at, at, ys.at[d], yr.at[d], tp=far)

    def across_in(d):
        at = dst.at[lax.rem(z + count - d, count), far_rows]
        return send(at, at, ys.at[d], yr.at[d], tp=far)

    def beside(d, second):
        at = dst.at[lax.rem(z + count - d, count), far_rows if second else mine]
        return send(at, at, cs.at[second, d], cr.at[second, d], tp=q ^ 1)

    for d in order:
        if d:
            hop(d).wait_recv()
        across(d).start()
        beside(d, 0).start()
    for d in order:
        across_in(d).wait_recv()
        beside(d, 1).start()
    for d in order:
        if d:
            hop(d).wait_send()
        across(d).wait_send()
        for second in (0, 1):
            beside(d, second).wait()
    for copy in keep:
        copy.wait()
    for e in range(extras):
        for d in range(1, count):
            hop_extra(e, d).wait()


def spread(src, extras, out_rows, extra_shapes, ident):
    count, _, width = src.shape
    sem = pltpu.SemaphoreType.DMA
    n = max(len(extras), 1)
    shapes = [jax.ShapeDtypeStruct((count, out_rows, width), src.dtype)]
    shapes += [jax.ShapeDtypeStruct(shape, x.dtype) for shape, x in zip(extra_shapes, extras)]
    return pl.pallas_call(
        functools.partial(spread_kernel, len(extras)),
        out_shape=shapes,
        in_specs=[pl.BlockSpec(memory_space=pltpu.VMEM)] * (1 + len(extras)),
        out_specs=[pl.BlockSpec(memory_space=pltpu.VMEM)] * (1 + len(extras)),
        scratch_shapes=[sem((1 + n,)), sem((count,)), sem((count,)), sem((count,)), sem((count,)),
                        sem((2, count)), sem((2, count)), sem((n, count)), sem((n, count))],
        compiler_params=pltpu.CompilerParams(collective_id=ident, has_side_effects=True),
        name="spread",
    )(src, *extras)


def swap_kernel(src_abs, dst_abs, src, dst, ss, rs, loc):
    q = lax.axis_index("tp")
    count = lax.axis_size("tp")
    meet([{"tp": q ^ r} for r in range(1, count)])

    def hop(r):
        return send(src.at[q ^ r if src_abs else r], dst.at[q if dst_abs else r], ss.at[r], rs.at[r], tp=q ^ r)

    for r in range(count - 1, 0, -1):
        hop(r).start()
    own = pltpu.make_async_copy(src.at[q if src_abs else 0], dst.at[q if dst_abs else 0], loc.at[0])
    own.start()
    own.wait()
    for r in range(1, count):
        hop(r).wait()


def swap(x, src_abs, dst_abs, ident):
    sem = pltpu.SemaphoreType.DMA
    count = x.shape[0]
    return pl.pallas_call(
        functools.partial(swap_kernel, src_abs, dst_abs),
        out_shape=jax.ShapeDtypeStruct(x.shape, x.dtype),
        in_specs=[pl.BlockSpec(memory_space=pltpu.VMEM)],
        out_specs=pl.BlockSpec(memory_space=pltpu.VMEM),
        scratch_shapes=[sem((count,)), sem((count,)), sem((1,))],
        compiler_params=pltpu.CompilerParams(collective_id=ident, has_side_effects=True),
        name="swap",
    )(x)


def fold_kernel(terms, out, near, relay, away, s1, r1, s2, r2):
    q = lax.axis_index("tp")
    count, _, _ = out.shape
    rows = out.shape[1]

    def quarter(p):
        return pl.ds(pl.multiple_of(p * rows, rows), rows)

    meet([{"tp": q ^ 1}, {"tp": q ^ 2}])

    def first(c, k):
        return send(terms.at[c, quarter(q ^ (3 if k else 1))], near.at[k, c], s1.at[k, c], r1.at[k, c], tp=q ^ 1)

    def second(c):
        return send(relay.at[c], away.at[c], s2.at[c], r2.at[c], tp=q ^ 2)

    for k in (1, 0):
        for c in range(count):
            first(c, k).start()
    for c in range(count):
        first(c, 1).wait_recv()
        relay[c] = (terms[c, quarter(q ^ 2), :].astype(F32) + near[1, c].astype(F32)).astype(BF)
        second(c).start()
    for c in range(count):
        first(c, 0).wait_recv()
        second(c).wait_recv()
        out[c] = terms[c, quarter(q), :].astype(F32) + near[0, c].astype(F32) + away[c].astype(F32)
    for c in range(count):
        first(c, 0).wait_send()
        first(c, 1).wait_send()
        second(c).wait_send()


def fold(terms, ident):
    count, n, width = terms.shape
    rows = n // lax.axis_size("tp")
    sem = pltpu.SemaphoreType.DMA
    return pl.pallas_call(
        fold_kernel,
        out_shape=jax.ShapeDtypeStruct((count, rows, width), F32),
        in_specs=[pl.BlockSpec(memory_space=pltpu.VMEM)],
        out_specs=pl.BlockSpec(memory_space=pltpu.VMEM),
        scratch_shapes=[pltpu.VMEM((2, count, rows, width), BF), pltpu.VMEM((count, rows, width), BF),
                        pltpu.VMEM((count, rows, width), BF), sem((2, count)), sem((2, count)), sem((count,)), sem((count,))],
        compiler_params=pltpu.CompilerParams(collective_id=ident, has_side_effects=True),
        name="fold",
    )(terms)


def norm(rows):
    mean = jnp.mean(rows, axis=-1, keepdims=True)
    centred = rows - mean
    inverse = lax.rsqrt(jnp.mean(centred * centred, axis=-1, keepdims=True) + NORM_EPS)
    return centred * inverse, inverse


def norm_back(grad, normed, inverse, gain):
    scaled = grad * gain
    return inverse * (
        scaled
        - jnp.mean(scaled, axis=-1, keepdims=True)
        - normed * jnp.mean(scaled * normed, axis=-1, keepdims=True)
    )


def middle_kernel(
    chunk, att, tok, te, affine, cot, w_out, w_in, w_down,
    out, gjs, gatt, g_out, g_in, g_down, sums, fl, sl, bl, act, gi, gp,
):
    slots = w_in.shape[0]
    n, width = tok.shape
    sums[...] = jnp.zeros_like(sums)

    def rows_step(j, carry):
        rows = pl.ds(pl.multiple_of(j * chunk, chunk), chunk)
        gain1, shift1 = affine[0:1, :], affine[1:2, :]
        gain2, shift2 = affine[2:3, :], affine[3:4, :]
        branch = contract(att[:, rows], w_out[...], 0, 0)
        normed1, inverse1 = norm(tok[rows, :].astype(F32) + te[...] + branch)
        first = normed1 * gain1 + shift1
        fl[rows, :] = first.astype(BF)
        second = first
        for t in range(slots):
            up, slope = gelu_pair(dot(fl[rows, :], w_in[t]))
            gp[t] = slope
            act[t, rows, :] = up.astype(BF)
            second += dot(act[t, rows, :], w_down[t])
        normed2, inverse2 = norm(second)
        out[rows, :] = (normed2 * gain2 + shift2).astype(BF)
        grad = cot[rows, :].astype(F32)
        sums[2:3, :] += jnp.sum(grad * normed2, axis=0, keepdims=True)
        sums[3:4, :] += jnp.sum(grad, axis=0, keepdims=True)
        grad = norm_back(grad, normed2, inverse2, gain2)
        sl[rows, :] = grad.astype(BF)
        for t in range(slots):
            gi[t, rows, :] = (contract(sl[rows, :], w_down[t], 1, 1) * gp[t]).astype(BF)
            grad += contract(gi[t, rows, :], w_in[t], 1, 1)
        sums[0:1, :] += jnp.sum(grad * normed1, axis=0, keepdims=True)
        sums[1:2, :] += jnp.sum(grad, axis=0, keepdims=True)
        grad = norm_back(grad, normed1, inverse1, gain1)
        gjs[rows, :] = grad
        bl[rows, :] = grad.astype(BF)
        gatt[:, rows] = contract(w_out[...], bl[rows, :], 1, 1).astype(BF)
        return carry

    lax.fori_loop(0, n // chunk, rows_step, 0)
    block = 256

    def slot_step(t, carry):
        for b in range(width // block):
            part = slice(b * block, (b + 1) * block)
            g_in[t, part, :] = contract(fl[:, part], gi[t], 0, 0).astype(BF)
        for b in range(w_down.shape[1] // block):
            part = slice(b * block, (b + 1) * block)
            g_down[t, part, :] = contract(act[t, :, part], sl[...], 0, 0).astype(BF)
        return carry

    lax.fori_loop(0, slots, slot_step, 0)
    for b in range(att.shape[0] // block):
        part = slice(b * block, (b + 1) * block)
        g_out[part, :] = dot(att[part, :], bl[...]).astype(BF)


def middle(att, tok, te, affine, cot, w_out, w_in, w_down, chunk=256):
    n, width = tok.shape
    slots, _, units = w_in.shape
    shape = jax.ShapeDtypeStruct
    vmem = pl.BlockSpec(memory_space=pltpu.VMEM)
    return pl.pallas_call(
        functools.partial(middle_kernel, chunk),
        out_shape=(
            shape((n, width), BF), shape((n, width), F32), shape(att.shape, BF),
            shape(w_out.shape, BF), shape(w_in.shape, BF), shape(w_down.shape, BF), shape((8, width), F32),
        ),
        in_specs=[vmem] * 8,
        out_specs=[vmem] * 7,
        scratch_shapes=[
            pltpu.VMEM((n, width), BF), pltpu.VMEM((n, width), BF), pltpu.VMEM((n, width), BF),
            pltpu.VMEM((slots, n, units), BF), pltpu.VMEM((slots, n, units), BF), pltpu.VMEM((slots, chunk, units), F32),
        ],
        name="middle",
        cost_estimate=pl.CostEstimate(
            flops=12 * n * width * (slots * units + width // 2), bytes_accessed=24 * slots * width * units, transcendentals=2 * n * slots * units
        ),
    )(att, tok, te, affine, cot, w_out, w_in, w_down)


def body(
    tokens, segments, timesteps, w_time1, w_time2, w_qkv, w_out, w_in, w_down, norm_gains, norm_shifts, cotangent
):
    seqs, length, width = tokens.shape
    shards, ctx, tp = lax.axis_size("shard"), lax.axis_size("ctx"), lax.axis_size("tp")
    x, z, q = lax.axis_index("shard"), lax.axis_index("ctx"), lax.axis_index("tp")
    if seqs != ctx or tp != 4:
        raise ValueError("unsupported mesh")
    rows = length // tp
    full = ctx * length
    heads = w_qkv.shape[2] // HEAD_DIM
    local = heads * HEAD_DIM

    def shard_gather(v):
        if shards == 2:
            other = lax.ppermute(v, "shard", [(0, 1), (1, 0)])
            return jnp.where(x == 0, jnp.stack([v, other]), jnp.stack([other, v]))
        return lax.all_gather(v, "shard", axis=0)

    def shard_sum(v):
        if shards == 2:
            return v + lax.ppermute(v, "shard", [(0, 1), (1, 0)])
        return lax.psum(v, "shard")

    def shard_scatter(v):
        if shards == 2:
            keep = lax.dynamic_index_in_dim(v, x, 0, keepdims=False)
            give = lax.dynamic_index_in_dim(v, 1 - x, 0, keepdims=False)
            return keep.astype(F32) + lax.ppermute(give, "shard", [(0, 1), (1, 0)]).astype(F32)
        return lax.psum_scatter(v, "shard", scatter_dimension=0, tiled=False).astype(F32)

    def tp_shift(v, bit):
        return lax.ppermute(v, "tp", [(i, i ^ bit) for i in range(tp)])

    token_rows, own_cot, seg = spread(
        tokens, [cotangent, segments.reshape(seqs, length // 128, 128)], length,
        [(ctx, rows, width), (ctx, length // 128, 128)], 0,
    )
    own_tok = lax.dynamic_slice_in_dim(token_rows, q * rows, rows, axis=1).reshape(ctx * rows, width)
    own_cot = own_cot.reshape(ctx * rows, width)
    seg = seg.reshape(full)

    pack = jnp.concatenate([w_out, w_in, w_down], axis=0)
    pair = shard_gather(pack)
    cuts = (0, w_out.shape[0], w_out.shape[0] + w_in.shape[0], pack.shape[0])
    base = jnp.concatenate([pair[:, cuts[i] : cuts[i + 1]].reshape(-1, width) for i in range(3)], axis=0)
    away = tp_shift(base, 2)
    slots = jnp.stack([base, tp_shift(base, 1), away, tp_shift(away, 1)])
    n_out, n_in, n_down = (shards * (cuts[i + 1] - cuts[i]) for i in range(3))
    out_w = slots[:, :n_out].reshape(tp * n_out, width)
    in_w = slots[:, n_out : n_out + n_in]
    down_w = slots[:, n_out + n_in :]
    qkv_w = shard_gather(w_qkv.reshape(-1, 3 * local)).reshape(width, 3 * local)
    affine = shard_gather(jnp.concatenate([norm_gains, norm_shifts], axis=1)).reshape(width, 4)
    affine = affine.astype(F32).T[jnp.array([0, 2, 1, 3])]

    feats = time_features(shard_gather(timesteps).reshape(-1), w_time1.shape[0] * shards).astype(BF)
    n1, n2 = w_time1.shape[0], w_time2.shape[0]
    own_feats = lax.dynamic_slice_in_dim(feats, x * n1, n1, axis=1)
    time_pre = shard_sum(dot(own_feats, w_time1))
    time_hidden = silu_fn(time_pre).astype(BF)
    own_hidden = lax.dynamic_slice_in_dim(time_hidden, x * n2, n2, axis=1)
    time_embed = shard_sum(dot(own_hidden, w_time2))
    te = lax.dynamic_slice_in_dim(time_embed, x * seqs + z, 1, axis=0)

    mixed_low = (token_rows.reshape(full, width).astype(F32) + te).astype(BF)
    joint_t = contract(qkv_w, mixed_low, 0, 1).astype(BF)
    joint_t = jnp.concatenate([joint_t[:local] * jnp.asarray(HEAD_DIM ** -0.5, BF), joint_t[local:]], axis=0)
    aq, ak = mask_rows(seg)
    lo, hi = key_ranges(seg, length, 512)
    att, lse = attend(joint_t, aq, ak, lo, hi, heads, HEAD_DIM, tp, length, 512)
    att_own = swap(att, True, False, 1).reshape(tp * local, ctx * rows)
    out_own, gjs, gatt, g_out, g_in, g_down, sums = middle(
        att_own, own_tok, te, affine, own_cot, out_w, in_w, down_w
    )
    (result,) = spread(out_own.reshape(ctx, rows, width), [], length, [], 2)
    got = swap(gatt.reshape(tp, local, ctx * rows), False, True, 3)
    lo, hi = key_ranges(seg, length, 256)
    dq, dkv = attend_back(joint_t, aq, ak, att, got, lse, lo, hi, heads, HEAD_DIM, tp, length, 256)
    grad_t = jnp.concatenate([dq, dkv], axis=0)
    g_qkv = contract(mixed_low, grad_t, 0, 1).astype(BF)
    terms = contract(grad_t, qkv_w, 0, 1).astype(BF).reshape(ctx, length, width)
    grad_own = gjs.reshape(ctx, rows, width) + fold(terms, 4)
    (grad_tokens,) = spread(grad_own.astype(BF), [], length, [], 5)

    total = jnp.zeros((seqs * shards, width), F32)
    total = lax.dynamic_update_slice_in_dim(total, jnp.sum(grad_own, axis=(0, 1))[None], x * seqs + z, 0)
    total = lax.psum(jnp.concatenate([total, sums[:4]], axis=0), ("shard", "ctx", "tp"))
    grad_embed = total[: seqs * shards].astype(BF)
    own_pre = lax.dynamic_slice_in_dim(time_pre, x * n2, n2, axis=1)
    grad_pre = jax.vjp(silu_fn, own_pre)[1](contract(grad_embed, w_time2, 1, 1))[0].astype(BF)
    grad_pre = jnp.swapaxes(shard_gather(grad_pre), 0, 1).reshape(seqs * shards, width)
    g_time1 = contract(own_feats, grad_pre, 0, 0)
    g_time2 = contract(own_hidden, grad_embed, 0, 0)
    share = width // shards
    affine_sums = lax.dynamic_slice_in_dim(total[seqs * shards :], x * share, share, axis=1)
    g_gains = jnp.stack([affine_sums[0], affine_sums[2]], axis=1)
    g_shifts = jnp.stack([affine_sums[1], affine_sums[3]], axis=1)

    grads = jnp.concatenate([g_out.reshape(tp, n_out, width), g_in, g_down], axis=1)
    near = tp_shift(jnp.stack([grads[1], grads[3]]), 1)
    half0 = (grads[0].astype(F32) + near[0].astype(F32))
    half2 = (grads[2].astype(F32) + near[1].astype(F32)).astype(BF)
    whole = (half0 + tp_shift(half2, 2).astype(F32)).astype(BF)
    marks = (0, n_out, n_out + n_in, n_out + n_in + n_down)
    whole = jnp.concatenate([whole[marks[i] : marks[i + 1]].reshape(shards, -1, width) for i in range(3)], axis=1)
    piece = shard_scatter(whole).astype(BF)
    qkv_piece = shard_scatter(g_qkv.reshape(shards, width // shards, 3 * local)).astype(BF)
    piece = lax.psum(piece, "ctx").astype(F32)
    qkv_piece = lax.psum(qkv_piece, "ctx").astype(F32)
    return (
        result, grad_tokens.astype(F32), g_time1, g_time2, qkv_piece.reshape(w_qkv.shape),
        piece[: cuts[1]], piece[cuts[1] : cuts[2]], piece[cuts[2] :], g_gains, g_shifts,
    )


def solution(mesh):
    placed = (
        P("shard", "ctx", None), P("shard", "ctx"), P("shard"), P("shard", None), P("shard", None),
        P("shard", None, "tp"), P(("tp", "shard"), None), P("shard", "tp"), P(("tp", "shard"), None),
        P("shard", None), P("shard", None), P("shard", "ctx", None),
    )
    return jax.shard_map(
        body,
        mesh=mesh,
        in_specs=placed,
        out_specs=(
            P("shard", "ctx", None), P("shard", "ctx", None), P("shard", None), P("shard", None),
            P("shard", None, "tp"), P(("tp", "shard"), None), P("shard", "tp"), P(("tp", "shard"), None),
            P("shard", None), P("shard", None),
        ),
        check_vma=False,
    )
```

```python
import functools
import math

import jax
import jax.numpy as jnp
from jax import lax
from jax.experimental import pallas as pl
from jax.experimental.pallas import tpu as pltpu
from jax.sharding import PartitionSpec as P

HEAD_DIM = 64
NORM_EPS = 1e-05
BIG = 1e30
BF = jnp.bfloat16
F32 = jnp.float32
MESH = pl.DeviceIdType.MESH


def time_features(steps_in, width):
    half = width // 2
    ratios = jnp.exp(-math.log(10000.0) * jnp.arange(half, dtype=F32) / half)
    angles = steps_in.astype(F32)[:, None] * ratios[None, :]
    return jnp.concatenate([jnp.cos(angles), jnp.sin(angles)], axis=1)


def silu_fn(value):
    return value / (1.0 + jnp.exp(-value))


def gelu_pair(v):
    half = 0.5 * (1.0 + lax.erf(v * (1.0 / math.sqrt(2.0))))
    bell = jnp.exp(-0.5 * v * v) * (1.0 / math.sqrt(2.0 * math.pi))
    return v * half, half + v * bell


def contract(left, right, ldim, rdim):
    return lax.dot_general(left, right, (((ldim,), (rdim,)), ((), ())), preferred_element_type=F32)


def dot(a, b):
    return contract(a, b, 1, 0)


def send(src, dst, send_sem, recv_sem, **where):
    return pltpu.make_async_remote_copy(
        src_ref=src, dst_ref=dst, send_sem=send_sem, recv_sem=recv_sem,
        device_id=where, device_id_type=MESH,
    )


def meet(peers):
    barrier = pltpu.get_barrier_semaphore()
    for where in peers:
        pl.semaphore_signal(barrier, inc=1, device_id=where, device_id_type=MESH)
    pl.semaphore_wait(barrier, len(peers))


def attend_kernel(heads, bk, lo_ref, hi_ref, qt_ref, kv_ref, aq_ref, ak_ref, ot_ref, lse_ref, ka, vat):
    i = pl.program_id(0)
    hd = qt_ref.shape[0] // heads
    parts, _, piece = ot_ref.shape
    each = range(heads)

    @pl.when(i == 0)
    def _():
        for h in each:
            ka[h] = jnp.concatenate([kv_ref[h * hd : (h + 1) * hd], ak_ref[...]], axis=0).T
            vat[h] = jnp.concatenate([kv_ref[(heads + h) * hd : (heads + h + 1) * hd], ak_ref[:16, :]], axis=0)

    bq = qt_ref.shape[1]
    qa = [jnp.concatenate([qt_ref[h * hd : (h + 1) * hd], aq_ref[...]], axis=0) for h in each]

    def step(j, carry):
        off = pl.multiple_of(j * bk, bk)
        s = [dot(ka[h, pl.ds(off, bk), :], qa[h]) for h in each]
        out = []
        for h in each:
            m, acc = carry[h]
            mn = jnp.maximum(m, jnp.max(s[h], axis=0, keepdims=True))
            p = jnp.exp(s[h] - mn).astype(BF)
            out.append((mn, acc * jnp.exp(m - mn) + dot(vat[h, :, pl.ds(off, bk)], p)))
        return tuple(out)

    m0 = jnp.full((1, bq), -BIG * 2, F32)
    a0 = jnp.zeros((hd + 16, bq), F32)
    done = lax.fori_loop(lo_ref[i], hi_ref[i], step, ((m0, a0),) * heads)
    for h in each:
        m, acc = done[h]
        total = acc[hd + 4 : hd + 5, :]
        out = (acc[:hd, :] / total).astype(BF)
        for t in range(parts):
            ot_ref[t, h * hd : (h + 1) * hd, :] = out[:, t * piece : (t + 1) * piece]
        lse_ref[h] = m + jnp.log(total)


def attend(joint_t, aq, ak, lo, hi, heads, hd, parts, bq, bk):
    n = joint_t.shape[1]
    w = heads * hd
    piece = bq // parts
    return pl.pallas_call(
        functools.partial(attend_kernel, heads, bk),
        out_shape=(
            jax.ShapeDtypeStruct((parts, w, n // parts), BF),
            jax.ShapeDtypeStruct((heads, 1, n), F32),
        ),
        grid_spec=pltpu.PrefetchScalarGridSpec(
            num_scalar_prefetch=2,
            grid=(n // bq,),
            in_specs=[
                pl.BlockSpec((w, bq), lambda i, *_: (0, i)),
                pl.BlockSpec((2 * w, n), lambda i, *_: (0, 0)),
                pl.BlockSpec((64, bq), lambda i, *_: (0, i)),
                pl.BlockSpec((64, n), lambda i, *_: (0, 0)),
            ],
            out_specs=[
                pl.BlockSpec((parts, w, piece), lambda i, *_: (0, 0, i)),
                pl.BlockSpec((heads, 1, bq), lambda i, *_: (0, 0, i)),
            ],
            scratch_shapes=[
                pltpu.VMEM((heads, n, hd + 64), BF),
                pltpu.VMEM((heads, hd + 16, n), BF),
            ],
        ),
        name="attend",
        cost_estimate=pl.CostEstimate(
            flops=4 * heads * n * n * hd, bytes_accessed=8 * heads * n * hd, transcendentals=heads * n * n
        ),
    )(lo, hi, joint_t[:w], joint_t[w:], aq, ak)


def split3(v):
    a = v.astype(BF)
    r = v - a.astype(F32)
    b = r.astype(BF)
    c = (r - b.astype(F32)).astype(BF)
    return a, b, c


def attend_back_kernel(
    heads, bk, scale, lo_ref, hi_ref, qt_ref, kv_ref, aq_ref, ak_ref, ot_ref, gt_ref, lse_ref,
    dq_ref, dkv_ref, ka, va, acc,
):
    i = pl.program_id(0)
    w, bq = qt_ref.shape
    parts = ot_ref.shape[0]
    hd = w // heads
    each = range(heads)

    @pl.when(i == 0)
    def _():
        for h in each:
            ka[h] = jnp.concatenate([kv_ref[h * hd : (h + 1) * hd], ak_ref[...]], axis=0).T
            va[h] = jnp.concatenate([kv_ref[(heads + h) * hd : (heads + h + 1) * hd], ak_ref[...]], axis=0).T
        acc[...] = jnp.zeros_like(acc)

    row = lax.broadcasted_iota(jnp.int32, (64, bq), 0)

    def rows3(v):
        a, b, c = split3(v)
        return (
            jnp.where(row == 4, a.astype(F32), 0.0)
            + jnp.where(row == 5, b.astype(F32), 0.0)
            + jnp.where(row == 6, c.astype(F32), 0.0)
        )

    qa, ga, right = [], [], []
    for h in each:
        part = slice(h * hd, (h + 1) * hd)
        qt = qt_ref[part]
        gt = jnp.concatenate([gt_ref[t, part, :] for t in range(parts)], axis=1)
        ot = jnp.concatenate([ot_ref[t, part, :] for t in range(parts)], axis=1)
        delta = jnp.sum(gt.astype(F32) * ot.astype(F32), axis=0, keepdims=True)
        qa.append(jnp.concatenate([qt, (aq_ref[...].astype(F32) + rows3(-lse_ref[h])).astype(BF)], axis=0))
        ga.append(jnp.concatenate([gt, rows3(-delta).astype(BF)], axis=0))
        zero = jnp.zeros_like(qt)
        right.append(
            jnp.concatenate(
                [jnp.concatenate([qt, zero], axis=0).T, jnp.concatenate([zero, gt], axis=0).T], axis=0
            )
        )

    def step(j, dq):
        off = pl.multiple_of(j * bk, bk)
        s = [dot(ka[h, pl.ds(off, bk), :], qa[h]) for h in each]
        g = [dot(va[h, pl.ds(off, bk), :], ga[h]) for h in each]
        out = []
        for h in each:
            p = jnp.exp(s[h])
            ds = (p * g[h]).astype(BF)
            acc[h, pl.ds(off, bk), :] += dot(jnp.concatenate([ds, p.astype(BF)], axis=1), right[h])
            out.append(dq[h] + dot(kv_ref[h * hd : (h + 1) * hd, pl.ds(off, bk)], ds))
        return tuple(out)

    dq = lax.fori_loop(lo_ref[i], hi_ref[i], step, (jnp.zeros((hd, bq), F32),) * heads)
    for h in each:
        dq_ref[h * hd : (h + 1) * hd] = (dq[h] * scale).astype(BF)

    @pl.when(i == pl.num_programs(0) - 1)
    def _():
        for h in each:
            full = acc[h].T
            dkv_ref[h * hd : (h + 1) * hd] = full[:hd].astype(BF)
            dkv_ref[(heads + h) * hd : (heads + h + 1) * hd] = full[hd:].astype(BF)


def attend_back(joint_t, aq, ak, ot, got, lse, lo, hi, heads, hd, parts, bq, bk):
    n = joint_t.shape[1]
    w = heads * hd
    piece = bq // parts
    return pl.pallas_call(
        functools.partial(attend_back_kernel, heads, bk, hd ** -0.5),
        out_shape=(jax.ShapeDtypeStruct((w, n), BF), jax.ShapeDtypeStruct((2 * w, n), BF)),
        grid_spec=pltpu.PrefetchScalarGridSpec(
            num_scalar_prefetch=2,
            grid=(n // bq,),
            in_specs=[
                pl.BlockSpec((w, bq), lambda i, *_: (0, i)),
                pl.BlockSpec((2 * w, n), lambda i, *_: (0, 0)),
                pl.BlockSpec((64, bq), lambda i, *_: (0, i)),
                pl.BlockSpec((64, n), lambda i, *_: (0, 0)),
                pl.BlockSpec((parts, w, piece), lambda i, *_: (0, 0, i)),
                pl.BlockSpec((parts, w, piece), lambda i, *_: (0, 0, i)),
                pl.BlockSpec((heads, 1, bq), lambda i, *_: (0, 0, i)),
            ],
            out_specs=[
                pl.BlockSpec((w, bq), lambda i, *_: (0, i)),
                pl.BlockSpec((2 * w, n), lambda i, *_: (0, 0)),
            ],
            scratch_shapes=[
                pltpu.VMEM((heads, n, hd + 64), BF),
                pltpu.VMEM((heads, n, hd + 64), BF),
                pltpu.VMEM((heads, n, 2 * hd), F32),
            ],
        ),
        name="attend_back",
        cost_estimate=pl.CostEstimate(
            flops=10 * heads * n * n * hd, bytes_accessed=16 * heads * n * hd, transcendentals=heads * n * n
        ),
    )(lo, hi, joint_t[:w], joint_t[w:], aq, ak, ot, got, lse)


def mask_rows(seg):
    n = seg.shape[0]
    one = seg[None, :] == jnp.arange(4, dtype=jnp.int32)[:, None]
    aq = jnp.concatenate([jnp.where(one, 0.0, -BIG).astype(BF), jnp.zeros((60, n), BF)], axis=0)
    ak = jnp.concatenate([one.astype(BF), jnp.ones((3, n), BF), jnp.zeros((57, n), BF)], axis=0)
    return aq, ak


def key_ranges(seg, bq, bk):
    first = seg[::bq]
    last = seg[bq - 1 :: bq]
    lo = jnp.sum(seg[None, :] < first[:, None], axis=1) // bk
    hi = (jnp.sum(seg[None, :] <= last[:, None], axis=1) + bk - 1) // bk
    return lo.astype(jnp.int32), hi.astype(jnp.int32)


def spread_kernel(extras, src, *refs):
    ins, dst, outs = refs[:extras], refs[extras], refs[extras + 1 : 2 * extras + 1]
    loc, zs, zr, ys, yr, cs, cr, es, er = refs[2 * extras + 1 :]
    z, q = lax.axis_index("ctx"), lax.axis_index("tp")
    count = lax.axis_size("ctx")
    wide = extras > 0
    rows = dst.shape[1] // lax.axis_size("tp")
    mine = pl.ds(pl.multiple_of(q * rows, rows), rows)
    far = q ^ 2
    far_rows = pl.ds(pl.multiple_of(far * rows, rows), rows)
    meet([{"ctx": lax.rem(z + d, count)} for d in range(1, count)] + [{"tp": q ^ 1}, {"tp": q ^ 2}])

    def hop(d):
        to = lax.rem(z + d, count)
        block = src.at[to, mine] if wide else src.at[to]
        return send(block, dst.at[z, mine], zs.at[d], zr.at[d], ctx=to)

    def part(ref, out, c):
        return ref.at[c] if ref.shape == out.shape else ref.at[c, mine]

    def hop_extra(e, d):
        to = lax.rem(z + d, count)
        return send(part(ins[e], outs[e], to), outs[e].at[z], es.at[e, d], er.at[e, d], ctx=to)

    for d in range(1, count):
        hop(d).start()
    if wide:
        keep = [pltpu.make_async_copy(src.at[z], dst.at[z], loc.at[0])]
        for e in range(extras):
            keep.append(pltpu.make_async_copy(part(ins[e], outs[e], z), outs[e].at[z], loc.at[e + 1]))
        for copy in keep:
            copy.start()
        for e in range(extras):
            for d in range(1, count):
                hop_extra(e, d).start()
        order = list(range(1, count))
    else:
        own = pltpu.make_async_copy(src.at[z], dst.at[z, mine], loc.at[0])
        own.start()
        own.wait()
        keep = []
        order = list(range(count))

    def across(d):
        at = dst.at[lax.rem(z + count - d, count), mine]
        return send(at, at, ys.at[d], yr.at[d], tp=far)

    def across_in(d):
        at = dst.at[lax.rem(z + count - d, count), far_rows]
        return send(at, at, ys.at[d], yr.at[d], tp=far)

    def beside(d, second):
        at = dst.at[lax.rem(z + count - d, count), far_rows if second else mine]
        return send(at, at, cs.at[second, d], cr.at[second, d], tp=q ^ 1)

    for d in order:
        if d:
            hop(d).wait_recv()
        across(d).start()
        beside(d, 0).start()
    for d in order:
        across_in(d).wait_recv()
        beside(d, 1).start()
    for d in order:
        if d:
            hop(d).wait_send()
        across(d).wait_send()
        for second in (0, 1):
            beside(d, second).wait()
    for copy in keep:
        copy.wait()
    for e in range(extras):
        for d in range(1, count):
            hop_extra(e, d).wait()


def spread(src, extras, out_rows, extra_shapes, ident):
    count, _, width = src.shape
    sem = pltpu.SemaphoreType.DMA
    n = max(len(extras), 1)
    shapes = [jax.ShapeDtypeStruct((count, out_rows, width), src.dtype)]
    shapes += [jax.ShapeDtypeStruct(shape, x.dtype) for shape, x in zip(extra_shapes, extras)]
    return pl.pallas_call(
        functools.partial(spread_kernel, len(extras)),
        out_shape=shapes,
        in_specs=[pl.BlockSpec(memory_space=pltpu.VMEM)] * (1 + len(extras)),
        out_specs=[pl.BlockSpec(memory_space=pltpu.VMEM)] * (1 + len(extras)),
        scratch_shapes=[sem((1 + n,)), sem((count,)), sem((count,)), sem((count,)), sem((count,)),
                        sem((2, count)), sem((2, count)), sem((n, count)), sem((n, count))],
        compiler_params=pltpu.CompilerParams(collective_id=ident, has_side_effects=True),
        name="spread",
    )(src, *extras)


def front_kernel(
    src, cot, seg, w_out, w_in, w_down, w_qkv, affine, feats, w_time1, w_time2,
    dst, own_cot, own_seg, out_w, in_w, down_w, qkv_w, affine_all, te, pre, hidden,
    feat, part1, part2, embed, hold_tok, hold_cot, hold_qkv, hold_out, hold_in, hold_down, loc, zs, zr, ss, rs,
):
    x, z, q = lax.axis_index("shard"), lax.axis_index("ctx"), lax.axis_index("tp")
    count = lax.axis_size("ctx")
    seqs = src.shape[0]
    rows = dst.shape[1] // lax.axis_size("tp")
    other, mate, far = 1 - x, q ^ 1, q ^ 2
    mine = pl.ds(pl.multiple_of(q * rows, rows), rows)
    far_rows = pl.ds(pl.multiple_of(far * rows, rows), rows)
    ids = iter(range(ss.shape[0]))
    every = []

    def remote(a, b, **where):
        i = next(ids)
        copy = send(a, b, ss.at[i], rs.at[i], **where)
        copy.start()
        every.append(copy)
        return copy

    to = ctx_peers(z, count)

    def hop(a, b, base, peer):
        return pltpu.make_async_remote_copy(
            src_ref=a, dst_ref=b, send_sem=zs.at[base, peer], recv_sem=zr.at[base, z],
            device_id={"ctx": peer}, device_id_type=MESH,
        )

    def landed(a, b, base, peer):
        return pltpu.make_async_remote_copy(
            src_ref=a, dst_ref=b, send_sem=zs.at[base, peer], recv_sem=zr.at[base, peer],
            device_id={"ctx": peer}, device_id_type=MESH,
        )

    pairs = [(src.at[z], hold_tok, dst.at[z]), (cot.at[z, mine], hold_cot, own_cot.at[z]),
             (w_qkv, hold_qkv, qkv_w.at[x]), (w_out, hold_out, out_w.at[0, x]),
             (w_in, hold_in, in_w.at[0, x]), (w_down, hold_down, down_w.at[0, x])]
    loads = [pltpu.make_async_copy(a, h, loc.at[0, i]) for i, (a, h, _) in enumerate(pairs)]
    keep = [pltpu.make_async_copy(h, b, loc.at[1, i]) for i, (_, h, b) in enumerate(pairs)]
    for copy in loads:
        copy.start()
    meet([{"ctx": p} for p in to] + [{"tp": mate}, {"tp": far}, {"shard": other}])
    feat[pl.ds(x, 1)] = feats[...][None]
    feat_in = remote(feats, feat.at[x], shard=other)
    for p in to:
        hop(seg.at[p], own_seg.at[z], 0, p).start()
    for p in to:
        hop(src.at[p, mine], dst.at[z, mine], 1, p).start()
    y_in = remote(w_in, in_w.at[2, x], tp=far)
    y_down = remote(w_down, down_w.at[2, x], tp=far)
    y_out = remote(w_out, out_w.at[2, x], tp=far)
    for p in to:
        hop(cot.at[p, mine], own_cot.at[z], 2, p).start()
    for piece, whole in ((w_out, out_w), (w_in, in_w), (w_down, down_w)):
        remote(piece, whole.at[1, x], tp=mate)
    own_seg[pl.ds(z, 1)] = seg[pl.ds(z, 1)]
    affine_all[pl.ds(x, 1)] = affine[...][None]
    for load, copy in zip(loads, keep):
        load.wait()
        copy.start()

    xf = x.astype(F32)
    feat_in.wait_recv()
    all_feats = jnp.concatenate([feat[0, :seqs], feat[1, :seqs]], axis=0)
    half = feats.shape[1] // 2
    own = (all_feats[:, :half] * (1.0 - xf) + all_feats[:, half:] * xf).astype(BF)
    part1[0] = dot(own, w_time1[...])
    part1_in = remote(part1.at[0], part1.at[1], shard=other)
    remote(w_qkv, qkv_w.at[x], shard=other)
    remote(affine, affine_all.at[x], shard=other)
    part1_in.wait_recv()
    pre[...] = part1[0] + part1[1]
    hid = silu_fn(pre[...])
    half = hid.shape[1] // 2
    own = (hid[:, :half] * (1.0 - xf) + hid[:, half:] * xf).astype(BF)
    hidden[...] = own
    part2[0] = dot(own, w_time2[...])
    part2_in = remote(part2.at[0], part2.at[1], shard=other)
    x_down = remote(w_down, down_w.at[0, x], shard=other)
    x_in = remote(w_in, in_w.at[0, x], shard=other)
    x_out = remote(w_out, out_w.at[0, x], shard=other)

    def pass_core(whole, slot, shard):
        remote(whole.at[slot, shard], whole.at[slot + 1, shard], tp=mate)

    across = []

    def pass_tokens(k):
        landed(src.at[to[k], mine], dst.at[to[k], mine], 1, to[k]).wait_recv()
        at = dst.at[to[k], mine]
        across.append(remote(at, at, tp=far))
        remote(at, at, tp=mate)

    pass_tokens(0)
    pass_tokens(1)
    y_in.wait_recv()
    diag_in = remote(in_w.at[2, x], in_w.at[2, x], shard=other)
    pass_core(in_w, 2, x)
    pass_tokens(2)
    x_down.wait_recv()
    diag_down = remote(down_w.at[0, other], down_w.at[2, other], tp=far)
    pass_core(down_w, 0, other)
    part2_in.wait_recv()
    embed[...] = part2[0] + part2[1]
    te[...] = embed[pl.ds(x * seqs + z, 1), :]
    y_down.wait_recv()
    pass_core(down_w, 2, x)
    y_out.wait_recv()
    diag_out = remote(out_w.at[2, x], out_w.at[2, x], shard=other)
    pass_core(out_w, 2, x)
    x_in.wait_recv()
    pass_core(in_w, 0, other)
    x_out.wait_recv()
    pass_core(out_w, 0, other)
    for k in range(len(to)):
        across[k].wait_recv()
        at = dst.at[to[k], far_rows]
        remote(at, at, tp=mate)
    diag_in.wait_recv()
    pass_core(in_w, 2, other)
    diag_down.wait_recv()
    pass_core(down_w, 2, other)
    diag_out.wait_recv()
    pass_core(out_w, 2, other)
    early = [feat_in, part1_in, part2_in, x_in, y_down, y_out, y_in, x_down, x_out, diag_in, diag_down, diag_out]
    early += across
    for copy in every:
        copy.wait_send()
        if all(copy is not e for e in early):
            copy.wait_recv()
    for p in to:
        hop(seg.at[p], own_seg.at[z], 0, p).wait_send()
        hop(src.at[p, mine], dst.at[z, mine], 1, p).wait_send()
        hop(cot.at[p, mine], own_cot.at[z], 2, p).wait_send()
        landed(seg.at[p], own_seg.at[p], 0, p).wait_recv()
        landed(cot.at[p, mine], own_cot.at[p], 2, p).wait_recv()
    for copy in keep:
        copy.wait()


def front(tokens, cot, seg, w_out, w_in, w_down, w_qkv, affine, feats, w_time1, w_time2, ident):
    seqs, length, width = tokens.shape
    count, tp = lax.axis_size("ctx"), lax.axis_size("tp")
    sem = pltpu.SemaphoreType.DMA
    shape = jax.ShapeDtypeStruct
    vmem = pl.BlockSpec(memory_space=pltpu.VMEM)
    hbm = pl.BlockSpec(memory_space=pl.ANY)
    time_rows = 2 * seqs
    outs = [
        shape((count, length, width), BF), shape((count, length // tp, width), BF), shape((count,) + seg.shape[1:], seg.dtype),
        shape((tp, 2) + w_out.shape, BF), shape((tp, 2) + w_in.shape, BF), shape((tp, 2) + w_down.shape, BF),
        shape((2,) + w_qkv.shape, BF), shape((2,) + affine.shape, F32),
        shape((1, width), F32), shape((time_rows, width), F32), shape((time_rows, w_time2.shape[0]), BF),
    ]
    return pl.pallas_call(
        front_kernel,
        out_shape=outs,
        in_specs=[hbm, hbm, vmem, hbm, hbm, hbm, hbm, vmem, vmem, vmem, vmem],
        out_specs=[hbm, hbm, vmem, hbm, hbm, hbm, hbm, vmem, vmem, vmem, vmem],
        scratch_shapes=[
            pltpu.VMEM((2,) + feats.shape, F32), pltpu.VMEM((2, time_rows, width), F32), pltpu.VMEM((2, time_rows, width), F32),
            pltpu.VMEM((time_rows, width), F32), pltpu.VMEM((length, width), BF), pltpu.VMEM((length // tp, width), BF),
            pltpu.VMEM(w_qkv.shape, BF), pltpu.VMEM(w_out.shape, BF), pltpu.VMEM(w_in.shape, BF), pltpu.VMEM(w_down.shape, BF),
            sem((2, 8)), sem((3, count)), sem((3, count)), sem((48,)), sem((48,)),
        ],
        compiler_params=pltpu.CompilerParams(collective_id=ident, has_side_effects=True),
        name="front",
    )(tokens, cot, seg, w_out, w_in, w_down, w_qkv, affine, feats, w_time1, w_time2)


def swap_kernel(src_abs, dst_abs, src, dst, ss, rs, loc):
    q = lax.axis_index("tp")
    count = lax.axis_size("tp")
    meet([{"tp": q ^ r} for r in range(1, count)])

    def hop(r):
        return send(src.at[q ^ r if src_abs else r], dst.at[q if dst_abs else r], ss.at[r], rs.at[r], tp=q ^ r)

    for r in range(count - 1, 0, -1):
        hop(r).start()
    own = pltpu.make_async_copy(src.at[q if src_abs else 0], dst.at[q if dst_abs else 0], loc.at[0])
    own.start()
    own.wait()
    for r in range(1, count):
        hop(r).wait()


def swap(x, src_abs, dst_abs, ident):
    sem = pltpu.SemaphoreType.DMA
    count = x.shape[0]
    return pl.pallas_call(
        functools.partial(swap_kernel, src_abs, dst_abs),
        out_shape=jax.ShapeDtypeStruct(x.shape, x.dtype),
        in_specs=[pl.BlockSpec(memory_space=pltpu.VMEM)],
        out_specs=pl.BlockSpec(memory_space=pltpu.VMEM),
        scratch_shapes=[sem((count,)), sem((count,)), sem((1,))],
        compiler_params=pltpu.CompilerParams(collective_id=ident, has_side_effects=True),
        name="swap",
    )(x)


def fold_kernel(terms, out, near, relay, away, s1, r1, s2, r2):
    q = lax.axis_index("tp")
    count, _, _ = out.shape
    rows = out.shape[1]

    def quarter(p):
        return pl.ds(pl.multiple_of(p * rows, rows), rows)

    meet([{"tp": q ^ 1}, {"tp": q ^ 2}])

    def first(c, k):
        return send(terms.at[c, quarter(q ^ (3 if k else 1))], near.at[k, c], s1.at[k, c], r1.at[k, c], tp=q ^ 1)

    def second(c):
        return send(relay.at[c], away.at[c], s2.at[c], r2.at[c], tp=q ^ 2)

    for k in (1, 0):
        for c in range(count):
            first(c, k).start()
    for c in range(count):
        first(c, 1).wait_recv()
        relay[c] = (terms[c, quarter(q ^ 2), :].astype(F32) + near[1, c].astype(F32)).astype(BF)
        second(c).start()
    for c in range(count):
        first(c, 0).wait_recv()
        second(c).wait_recv()
        out[c] = terms[c, quarter(q), :].astype(F32) + near[0, c].astype(F32) + away[c].astype(F32)
    for c in range(count):
        first(c, 0).wait_send()
        first(c, 1).wait_send()
        second(c).wait_send()


def fold(terms, ident):
    count, n, width = terms.shape
    rows = n // lax.axis_size("tp")
    sem = pltpu.SemaphoreType.DMA
    return pl.pallas_call(
        fold_kernel,
        out_shape=jax.ShapeDtypeStruct((count, rows, width), F32),
        in_specs=[pl.BlockSpec(memory_space=pltpu.VMEM)],
        out_specs=pl.BlockSpec(memory_space=pltpu.VMEM),
        scratch_shapes=[pltpu.VMEM((2, count, rows, width), BF), pltpu.VMEM((count, rows, width), BF),
                        pltpu.VMEM((count, rows, width), BF), sem((2, count)), sem((2, count)), sem((count,)), sem((count,))],
        compiler_params=pltpu.CompilerParams(collective_id=ident, has_side_effects=True),
        name="fold",
    )(terms)


def ctx_peers(z, count):
    if count != 4:
        return tuple(lax.rem(z + d, count) for d in range(1, count))
    upper = z // 2
    return z ^ 1, 2 - upper, 3 - 3 * upper


def add_rows(out, terms, step=96):
    def body(i, carry):
        r = pl.ds(pl.multiple_of(i * step, step), step)
        total = terms[0][r, :].astype(F32)
        for t in terms[1:]:
            total = total + t[r, :].astype(F32)
        out[r, :] = total.astype(out.dtype)
        return carry

    lax.fori_loop(0, out.shape[0] // step, body, 0)


def turn_kernel(
    gatt, g_out, g_in, g_down, got, send_y, keep_y, send_x, keep_x,
    hold, own_out, own_in, own_down, near_out, near_in, near_down, loc, ss, rs,
):
    x, q = lax.axis_index("shard"), lax.axis_index("tp")
    ids = iter(range(ss.shape[0]))
    every = []

    def remote(a, b, **where):
        i = next(ids)
        copy = send(a, b, ss.at[i], rs.at[i], **where)
        copy.start()
        every.append(copy)
        return copy

    pairs = [(gatt.at[0], hold)]
    for i, t in ((0, 0), (1, 2)):
        pairs += [(g_in.at[t], own_in.at[i]), (g_out.at[t], own_out.at[i]), (g_down.at[t], own_down.at[i])]
    loads = [pltpu.make_async_copy(a, b, loc.at[i]) for i, (a, b) in enumerate(pairs)]
    for copy in loads:
        copy.start()
    meet([{"tp": q ^ r} for r in (1, 2, 3)])
    for r in (2, 3, 1):
        remote(gatt.at[r], got.at[q], tp=q ^ r)
    come_in = [remote(g_in.at[t], near_in.at[i], tp=q ^ 1) for i, t in ((1, 3), (0, 1))]
    come_out = [remote(g_out.at[t], near_out.at[i], tp=q ^ 1) for i, t in ((1, 3), (0, 1))]
    come_down = [remote(g_down.at[t], near_down.at[i], tp=q ^ 1) for i, t in ((1, 3), (0, 1))]
    for copy in loads:
        copy.wait()
    own = pltpu.make_async_copy(hold, got.at[q], loc.at[len(pairs)])
    own.start()
    come_in[0].wait_recv()
    add_rows(send_y, (own_in.at[1], near_in.at[1]))
    for copy in come_out + come_down:
        copy.wait_recv()
    n_out, n_down = own_out.shape[1] // 2, own_down.shape[1] // 2
    for i in (1, 0):
        for shard, to in ((1 - x, send_x), (x, keep_x)):
            r = pl.ds(pl.multiple_of(shard * n_out, n_out), n_out)
            add_rows(to.at[i, pl.ds(0, n_out)], (own_out.at[i, r], near_out.at[i, r]))
            r = pl.ds(pl.multiple_of(shard * n_down, n_down), n_down)
            add_rows(to.at[i, pl.ds(n_out, n_down)], (own_down.at[i, r], near_down.at[i, r]))
    come_in[1].wait_recv()
    add_rows(keep_y, (own_in.at[0], near_in.at[0]))
    for i, copy in enumerate(every):
        copy.wait_send()
        if i < 3:
            copy.wait_recv()
    own.wait()


def turn(gatt, g_out, g_in, g_down, ident):
    sem = pltpu.SemaphoreType.DMA
    shape = jax.ShapeDtypeStruct
    vmem, hbm = pl.BlockSpec(memory_space=pltpu.VMEM), pl.BlockSpec(memory_space=pl.ANY)
    width = g_in.shape[2]
    both = shape((2, (g_out.shape[1] + g_down.shape[1]) // 2, width), BF)
    two = lambda w: pltpu.VMEM((2,) + w.shape[1:], BF)
    return pl.pallas_call(
        turn_kernel,
        out_shape=(shape(gatt.shape, BF), shape(g_in.shape[1:], BF), shape(g_in.shape[1:], BF), both, both),
        in_specs=[hbm] * 4,
        out_specs=[hbm, vmem, vmem, vmem, vmem],
        scratch_shapes=[pltpu.VMEM(gatt.shape[1:], BF)] + [two(w) for w in (g_out, g_in, g_down)] * 2
        + [sem((8,)), sem((9,)), sem((9,))],
        compiler_params=pltpu.CompilerParams(collective_id=ident, has_side_effects=True),
        name="turn",
    )(gatt, g_out, g_in, g_down)


def tail_kernel(
    chunks, terms, gjs, sums, own_out, in_y, keep_y, in_x, keep_x, g_qkv,
    result, gtok, o_in, o_both, o_qkv, totals,
    tq, near, relay, away, low, x_give, x_take, y_give, y_take, qkv_take, m_in, m_both, m_qkv,
    box_in, box_both, box_qkv, mid_in, mid_both, mid_qkv, f_in, f_both, f_qkv,
    small, small_tp, small_z, small_x, loc, zs, zr, cs, cr, ss, rs,
):
    x, z, q = lax.axis_index("shard"), lax.axis_index("ctx"), lax.axis_index("tp")
    count, rows, width = own_out.shape
    other, mate, far = 1 - x, q ^ 1, q ^ 2
    mine = pl.ds(pl.multiple_of(q * rows, rows), rows)
    far_rows = pl.ds(pl.multiple_of(far * rows, rows), rows)
    ids = iter(range(ss.shape[0]))
    every, early = [], []

    def quarter(p):
        return pl.ds(pl.multiple_of(p * rows, rows), rows)

    def remote(a, b, **where):
        i = next(ids)
        copy = send(a, b, ss.at[i], rs.at[i], **where)
        copy.start()
        every.append(copy)
        return copy

    def arrive(copy):
        copy.wait_recv()
        early.append(copy)

    to = ctx_peers(z, count)

    def hop(a, b, base, peer):
        return send(a, b, zs.at[base, peer], zr.at[base, z], ctx=peer)

    def landed(b, base, peer):
        return send(b, b, zs.at[base, peer], zr.at[base, peer], ctx=peer)

    load_far = pltpu.make_async_copy(terms.at[:, quarter(far)], tq.at[1], loc.at[0])
    load_own = pltpu.make_async_copy(terms.at[:, quarter(q)], tq.at[0], loc.at[1])
    load_far.start()
    load_own.start()
    meet([{"ctx": p} for p in to] + [{"tp": q ^ r} for r in (1, 2, 3)] + [{"shard": other}])

    near_far = [remote(terms.at[c, quarter(q ^ 3)], near.at[1, c], tp=mate) for c in range(count)]
    near_own = [remote(terms.at[c, quarter(mate)], near.at[0, c], tp=mate) for c in range(count)]
    qkv_in = remote(g_qkv.at[other], qkv_take, shard=other)
    for p in to:
        hop(own_out.at[p], result.at[z, mine], 0, p).start()
    put_out = pltpu.make_async_copy(own_out.at[z], result.at[z, mine], loc.at[2])
    put_out.start()
    load_far.wait()
    from_far = []
    for c in range(count):
        arrive(near_far[c])
        relay[c] = (tq[1, c].astype(F32) + near[1, c].astype(F32)).astype(BF)
        from_far.append(remote(relay.at[c], away.at[c], tp=far))
    n_in, n_both = x_give.shape[0], y_give.shape[0]
    give = pl.ds(pl.multiple_of(other * n_in, n_in), n_in)
    keep = pl.ds(pl.multiple_of(x * n_in, n_in), n_in)
    add_rows(x_give, (keep_y.at[give], in_y.at[give]))
    x_in = remote(x_give, x_take, shard=other)
    add_rows(y_give, (keep_x.at[1], in_x.at[1]))
    y_in = remote(y_give, y_take, tp=far)

    def share(ref, base, own):
        blocks = [remote(own, ref.at[z, mine], tp=far)]
        remote(own, ref.at[z, mine], tp=mate)

        def step(k):
            at = ref.at[to[k], mine]
            landed(at, base, to[k]).wait_recv()
            blocks.append(remote(at, at, tp=far))
            remote(at, at, tp=mate)

        def finish(k):
            arrive(blocks[k])
            at = ref.at[z if k == 0 else to[k - 1], far_rows]
            remote(at, at, tp=mate)

        return step, finish

    out_step, out_finish = share(result, 0, own_out.at[z])
    load_own.wait()
    column = jnp.zeros((1, width), F32)
    for c in range(count):
        arrive(near_own[c])
        arrive(from_far[c])
        grad = gjs[c * rows : (c + 1) * rows, :] + tq[0, c].astype(F32) + near[0, c].astype(F32) + away[c].astype(F32)
        low[c] = grad.astype(BF)
        column = column + jnp.sum(grad, axis=0, keepdims=True)
    for p in to:
        hop(low.at[p], gtok.at[z, mine], 1, p).start()
    put_tok = pltpu.make_async_copy(low.at[z], gtok.at[z, mine], loc.at[3])
    put_tok.start()
    seqs = (totals.shape[0] - 8) // 2
    small[0] = jnp.zeros(small.shape[1:], F32)
    small[0, pl.ds(x * seqs + z, 1), :] = column
    small[0, 2 * seqs : 2 * seqs + 4, :] = sums[0:4, :]
    small_tp[pl.ds(q, 1)] = small[0][None]
    tp_small = [remote(small.at[0], small_tp.at[q], tp=q ^ r) for r in (1, 2, 3)]
    tok_step, tok_finish = share(gtok, 1, low.at[z])
    for k in range(count - 1):
        out_step(k)

    arrive(qkv_in)
    add_rows(m_qkv, (g_qkv.at[x], qkv_take))
    inner = (z == 1) | (z == 2)
    outer = (z == 0) | (z == 3)
    sets = {"qkv": (m_qkv, box_qkv, mid_qkv, f_qkv, o_qkv), "in": (m_in, box_in, mid_in, f_in, o_in),
            "both": (m_both, box_both, mid_both, f_both, o_both)}
    plan = []
    for name in ("qkv", "in", "both"):
        total = sets[name][0].shape[0]
        step = chunks[name]
        for i in range(total // step):
            plan.append((sets[name], pl.ds(i * step, step)))

    def toward(k):
        (m, box, _, _, _), r = plan[k]
        return send(m.at[r], box.at[r], cs.at[0, k], cr.at[0, k], ctx=z ^ 1)

    def across(k):
        (m, _, mid, _, _), r = plan[k]
        return send(m.at[r], mid.at[r], cs.at[1, k], cr.at[1, k], ctx=3 - z)

    def back(k):
        (_, _, _, f, _), r = plan[k]
        return send(f.at[r], f.at[r], cs.at[2, k], cr.at[2, k], ctx=z ^ 1)

    def begin(k):
        @pl.when(outer)
        def _():
            toward(k).start()

    def join(k):
        @pl.when(inner)
        def _():
            (m, box, _, _, _), r = plan[k]
            toward(k).wait_recv()
            add_rows(m.at[r], (m.at[r], box.at[r]))
            across(k).start()

    def settle(k):
        @pl.when(inner)
        def _():
            (m, _, mid, f, _), r = plan[k]
            across(k).wait_recv()
            add_rows(f.at[r], (m.at[r], mid.at[r]))
            back(k).start()

    first_in = sum(1 for entry in plan if entry[0] is sets["qkv"])
    first_both = first_in + sum(1 for entry in plan if entry[0] is sets["in"])
    last = len(plan)
    for k in range(first_in):
        begin(k)
    arrive(x_in)
    add_rows(m_in, (keep_y.at[keep], in_y.at[keep], x_take))
    for k in range(first_in, first_both):
        begin(k)
    arrive(y_in)
    add_rows(m_both, (keep_x.at[0], in_x.at[0], y_take))
    for k in range(first_both, last):
        begin(k)
    for copy in tp_small:
        arrive(copy)
    small[1] = small_tp[0] + small_tp[1] + small_tp[2] + small_tp[3]
    small_z[pl.ds(z, 1)] = small[1][None]
    for p in to:
        hop(small.at[1], small_z.at[z], 2, p).start()
    join(0)
    for k in range(1, last):
        join(k)
        settle(k - 1)
        if k == 2:
            for j in range(count):
                out_finish(j)
        if k in (3, 4, 5):
            tok_step(k - 3)
        if k == 5:
            for p in to:
                landed(small_z.at[p], 2, p).wait_recv()
            small[2] = small_z[0] + small_z[1] + small_z[2] + small_z[3]
            small_x[pl.ds(x, 1)] = small[2][None]
            x_small = remote(small.at[2], small_x.at[x], shard=other)
    settle(last - 1)
    for k in range(count):
        tok_finish(k)
    arrive(x_small)
    totals[...] = small_x[0] + small_x[1]
    for k in range(last):
        (_, _, _, f, o), r = plan[k]

        @pl.when(outer)
        def _():
            back(k).wait_recv()

        add_rows(o.at[r], (f.at[r],))
    for k in range(last):
        @pl.when(outer)
        def _():
            toward(k).wait_send()

        @pl.when(inner)
        def _():
            across(k).wait_send()
            back(k).wait_send()
    for copy in every:
        copy.wait_send()
        if all(copy is not e for e in early):
            copy.wait_recv()
    for p in to:
        hop(own_out.at[p], result.at[z, mine], 0, p).wait_send()
        hop(low.at[p], gtok.at[z, mine], 1, p).wait_send()
        hop(small.at[1], small_z.at[z], 2, p).wait_send()
    put_out.wait()
    put_tok.wait()


def tail(terms, gjs, sums, own_out, in_y, keep_y, in_x, keep_x, g_qkv, seqs, ident):
    count, length, width = terms.shape
    rows = own_out.shape[1]
    sem = pltpu.SemaphoreType.DMA
    shape = jax.ShapeDtypeStruct
    vmem, hbm = pl.BlockSpec(memory_space=pltpu.VMEM), pl.BlockSpec(memory_space=pl.ANY)
    n_in, n_both, n_qkv = (in_y.shape[0] // 2, width), in_x.shape[1:], g_qkv.shape[1:]
    three = (n_in, n_both, n_qkv)
    small = (2 * seqs + 8, width)
    low = lambda *s: pltpu.VMEM(s, BF)
    return pl.pallas_call(
        functools.partial(tail_kernel, {"qkv": n_qkv[0] // 2, "in": n_in[0] // 2, "both": n_both[0] // 5}),
        out_shape=(
            shape((count, length, width), BF), shape((count, length, width), BF),
            shape(n_in, F32), shape(n_both, F32), shape(n_qkv, F32), shape(small, F32),
        ),
        in_specs=[hbm] + [vmem] * 8,
        out_specs=[hbm, hbm, vmem, vmem, vmem, vmem],
        scratch_shapes=[
            low(2, count, rows, width), low(2, count, rows, width), low(count, rows, width), low(count, rows, width),
            low(count, rows, width), low(*n_in), low(*n_in), low(*n_both), low(*n_both), low(*n_qkv),
        ] + [low(*n) for n in three] * 4 + [
            pltpu.VMEM((3,) + small, F32), pltpu.VMEM((4,) + small, F32), pltpu.VMEM((count,) + small, F32), pltpu.VMEM((2,) + small, F32),
            sem((4,)), sem((3, count)), sem((3, count)), sem((3, 16)), sem((3, 16)), sem((48,)), sem((48,)),
        ],
        compiler_params=pltpu.CompilerParams(collective_id=ident, has_side_effects=True),
        name="tail",
    )(terms, gjs, sums, own_out, in_y, keep_y, in_x, keep_x, g_qkv)


def norm(rows):
    mean = jnp.mean(rows, axis=-1, keepdims=True)
    centred = rows - mean
    inverse = lax.rsqrt(jnp.mean(centred * centred, axis=-1, keepdims=True) + NORM_EPS)
    return centred * inverse, inverse


def norm_back(grad, normed, inverse, gain):
    scaled = grad * gain
    return inverse * (
        scaled
        - jnp.mean(scaled, axis=-1, keepdims=True)
        - normed * jnp.mean(scaled * normed, axis=-1, keepdims=True)
    )


def middle_kernel(
    chunk, att, tok, te, affine, cot, w_out, w_in, w_down,
    out, gjs, gatt, g_out, g_in, g_down, sums, fl, sl, bl, act, gi, gp,
):
    slots = w_in.shape[0]
    n, width = tok.shape
    sums[...] = jnp.zeros_like(sums)

    def rows_step(j, carry):
        rows = pl.ds(pl.multiple_of(j * chunk, chunk), chunk)
        gain1, shift1 = affine[0:1, :], affine[1:2, :]
        gain2, shift2 = affine[2:3, :], affine[3:4, :]
        branch = contract(att[:, rows], w_out[...], 0, 0)
        normed1, inverse1 = norm(tok[rows, :].astype(F32) + te[...] + branch)
        first = normed1 * gain1 + shift1
        fl[rows, :] = first.astype(BF)
        second = first
        for t in range(slots):
            up, slope = gelu_pair(dot(fl[rows, :], w_in[t]))
            gp[t] = slope
            act[t, rows, :] = up.astype(BF)
            second += dot(act[t, rows, :], w_down[t])
        normed2, inverse2 = norm(second)
        out[rows, :] = (normed2 * gain2 + shift2).astype(BF)
        grad = cot[rows, :].astype(F32)
        sums[2:3, :] += jnp.sum(grad * normed2, axis=0, keepdims=True)
        sums[3:4, :] += jnp.sum(grad, axis=0, keepdims=True)
        grad = norm_back(grad, normed2, inverse2, gain2)
        sl[rows, :] = grad.astype(BF)
        for t in range(slots):
            gi[t, rows, :] = (contract(sl[rows, :], w_down[t], 1, 1) * gp[t]).astype(BF)
            grad += contract(gi[t, rows, :], w_in[t], 1, 1)
        sums[0:1, :] += jnp.sum(grad * normed1, axis=0, keepdims=True)
        sums[1:2, :] += jnp.sum(grad, axis=0, keepdims=True)
        grad = norm_back(grad, normed1, inverse1, gain1)
        gjs[rows, :] = grad
        bl[rows, :] = grad.astype(BF)
        gatt[:, rows] = contract(w_out[...], bl[rows, :], 1, 1).astype(BF)
        return carry

    lax.fori_loop(0, n // chunk, rows_step, 0)
    block = 256

    def slot_step(t, carry):
        for b in range(width // block):
            part = slice(b * block, (b + 1) * block)
            g_in[t, part, :] = contract(fl[:, part], gi[t], 0, 0).astype(BF)
        for b in range(w_down.shape[1] // block):
            part = slice(b * block, (b + 1) * block)
            g_down[t, part, :] = contract(act[t, :, part], sl[...], 0, 0).astype(BF)
        return carry

    lax.fori_loop(0, slots, slot_step, 0)
    for b in range(att.shape[0] // block):
        part = slice(b * block, (b + 1) * block)
        g_out[part, :] = dot(att[part, :], bl[...]).astype(BF)


def middle(att, tok, te, affine, cot, w_out, w_in, w_down, chunk=256):
    n, width = tok.shape
    slots, _, units = w_in.shape
    shape = jax.ShapeDtypeStruct
    vmem = pl.BlockSpec(memory_space=pltpu.VMEM)
    return pl.pallas_call(
        functools.partial(middle_kernel, chunk),
        out_shape=(
            shape((n, width), BF), shape((n, width), F32), shape(att.shape, BF),
            shape(w_out.shape, BF), shape(w_in.shape, BF), shape(w_down.shape, BF), shape((8, width), F32),
        ),
        in_specs=[vmem] * 8,
        out_specs=[vmem] * 7,
        scratch_shapes=[
            pltpu.VMEM((n, width), BF), pltpu.VMEM((n, width), BF), pltpu.VMEM((n, width), BF),
            pltpu.VMEM((slots, n, units), BF), pltpu.VMEM((slots, n, units), BF), pltpu.VMEM((slots, chunk, units), F32),
        ],
        name="middle",
        cost_estimate=pl.CostEstimate(
            flops=12 * n * width * (slots * units + width // 2), bytes_accessed=24 * slots * width * units, transcendentals=2 * n * slots * units
        ),
    )(att, tok, te, affine, cot, w_out, w_in, w_down)


def body(
    tokens, segments, timesteps, w_time1, w_time2, w_qkv, w_out, w_in, w_down, norm_gains, norm_shifts, cotangent
):
    seqs, length, width = tokens.shape
    shards, ctx, tp = lax.axis_size("shard"), lax.axis_size("ctx"), lax.axis_size("tp")
    x, z, q = lax.axis_index("shard"), lax.axis_index("ctx"), lax.axis_index("tp")
    if seqs != ctx or tp != 4:
        raise ValueError("unsupported mesh")
    rows = length // tp
    full = ctx * length
    heads = w_qkv.shape[2] // HEAD_DIM
    local = heads * HEAD_DIM

    def shard_gather(v):
        if shards == 2:
            other = lax.ppermute(v, "shard", [(0, 1), (1, 0)])
            return jnp.where(x == 0, jnp.stack([v, other]), jnp.stack([other, v]))
        return lax.all_gather(v, "shard", axis=0)

    def shard_sum(v):
        if shards == 2:
            return v + lax.ppermute(v, "shard", [(0, 1), (1, 0)])
        return lax.psum(v, "shard")

    def shard_scatter(v):
        if shards == 2:
            keep = lax.dynamic_index_in_dim(v, x, 0, keepdims=False)
            give = lax.dynamic_index_in_dim(v, 1 - x, 0, keepdims=False)
            return keep.astype(F32) + lax.ppermute(give, "shard", [(0, 1), (1, 0)]).astype(F32)
        return lax.psum_scatter(v, "shard", scatter_dimension=0, tiled=False).astype(F32)

    def tp_shift(v, bit):
        return lax.ppermute(v, "tp", [(i, i ^ bit) for i in range(tp)])

    n_out, n_in, n_down = (shards * w.shape[0] for w in (w_out, w_in, w_down))
    cuts = (0, w_out.shape[0], w_out.shape[0] + w_in.shape[0], w_out.shape[0] + w_in.shape[0] + w_down.shape[0])
    n1, n2 = w_time1.shape[0], w_time2.shape[0]
    blocks = segments.reshape(seqs, length // 128, 128)
    qkv_flat = w_qkv.reshape(-1, 3 * local)
    pairs = jnp.concatenate([norm_gains, norm_shifts], axis=1).astype(F32)
    if shards == 2:
        feats = time_features(timesteps, n1 * shards).astype(BF).astype(F32)
        rows8 = jnp.zeros((8, n1 * shards), F32).at[:seqs].set(feats)
        affine = jnp.zeros((8, n2), F32).at[:4].set(pairs.T[jnp.array([0, 2, 1, 3])])
        token_rows, own_cot, seg, out_w, in_w, down_w, qkv_w, affine, te, time_pre, own_hidden = front(
            tokens, cotangent, blocks, w_out, w_in, w_down, qkv_flat, affine, rows8, w_time1, w_time2, 0
        )
        feats = shard_gather(feats).reshape(-1, n1 * shards).astype(BF)
        own_feats = lax.dynamic_slice_in_dim(feats, x * n1, n1, axis=1)
        out_w = out_w.reshape(tp * n_out, width)
        in_w = in_w.reshape(tp, n_in, width)
        down_w = down_w.reshape(tp, n_down, width)
        qkv_w = qkv_w.reshape(width, 3 * local)
        affine = jnp.concatenate([affine[0], affine[1]], axis=1)
    else:
        token_rows, own_cot, seg = spread(
            tokens, [cotangent, blocks], length, [(ctx, rows, width), (ctx, length // 128, 128)], 0,
        )
        base = jnp.concatenate([shard_gather(w).reshape(-1, width) for w in (w_out, w_in, w_down)], axis=0)
        away = tp_shift(base, 2)
        slots = jnp.stack([base, tp_shift(base, 1), away, tp_shift(away, 1)])
        out_w = slots[:, :n_out].reshape(tp * n_out, width)
        in_w = slots[:, n_out : n_out + n_in]
        down_w = slots[:, n_out + n_in :]
        qkv_w = shard_gather(qkv_flat).reshape(width, 3 * local)
        affine = shard_gather(pairs).reshape(width, 4).T[jnp.array([0, 2, 1, 3])]
        feats = time_features(shard_gather(timesteps).reshape(-1), n1 * shards).astype(BF)
        own_feats = lax.dynamic_slice_in_dim(feats, x * n1, n1, axis=1)
        time_pre = shard_sum(dot(own_feats, w_time1))
        time_hidden = silu_fn(time_pre).astype(BF)
        own_hidden = lax.dynamic_slice_in_dim(time_hidden, x * n2, n2, axis=1)
        time_embed = shard_sum(dot(own_hidden, w_time2))
        te = lax.dynamic_slice_in_dim(time_embed, x * seqs + z, 1, axis=0)
    own_tok = lax.dynamic_slice_in_dim(token_rows, q * rows, rows, axis=1).reshape(ctx * rows, width)
    own_cot = own_cot.reshape(ctx * rows, width)
    seg = seg.reshape(full)

    mixed_low = (token_rows.reshape(full, width).astype(F32) + te).astype(BF)
    joint_t = contract(qkv_w, mixed_low, 0, 1).astype(BF)
    joint_t = jnp.concatenate([joint_t[:local] * jnp.asarray(HEAD_DIM ** -0.5, BF), joint_t[local:]], axis=0)
    aq, ak = mask_rows(seg)
    lo, hi = key_ranges(seg, length, 512)
    att, lse = attend(joint_t, aq, ak, lo, hi, heads, HEAD_DIM, tp, length, 512)
    att_own = swap(att, True, False, 1).reshape(tp * local, ctx * rows)
    out_own, gjs, gatt, g_out, g_in, g_down, sums = middle(
        att_own, own_tok, te, affine, own_cot, out_w, in_w, down_w
    )
    out_own = out_own.reshape(ctx, rows, width)
    gatt = gatt.reshape(tp, local, ctx * rows)
    g_out = g_out.reshape(tp, n_out, width)
    fast = shards == 2 and ctx == 4
    if fast:
        got, send_y, keep_y, send_x, keep_x = turn(gatt, g_out, g_in, g_down, 3)
        in_y = tp_shift(send_y, 2)
        in_x = lax.ppermute(send_x, "shard", [(0, 1), (1, 0)])
    else:
        (result,) = spread(out_own, [], length, [], 2)
        got = swap(gatt, False, True, 3)
    lo, hi = key_ranges(seg, length, 256)
    dq, dkv = attend_back(joint_t, aq, ak, att, got, lse, lo, hi, heads, HEAD_DIM, tp, length, 256)
    grad_t = jnp.concatenate([dq, dkv], axis=0)
    g_qkv = contract(mixed_low, grad_t, 0, 1).astype(BF)
    terms = contract(grad_t, qkv_w, 0, 1).astype(BF).reshape(ctx, length, width)
    if fast:
        result, grad_tokens, piece_in, piece_both, qkv_piece, total = tail(
            terms, gjs, sums, out_own, in_y, keep_y, in_x, keep_x, g_qkv.reshape(shards, width // shards, 3 * local), seqs, 4
        )
        total = total[: seqs * shards + 4]
    else:
        grad_own = gjs.reshape(ctx, rows, width) + fold(terms, 4)
        (grad_tokens,) = spread(grad_own.astype(BF), [], length, [], 5)
        total = jnp.zeros((seqs * shards, width), F32)
        total = lax.dynamic_update_slice_in_dim(total, jnp.sum(grad_own, axis=(0, 1))[None], x * seqs + z, 0)
        total = lax.psum(jnp.concatenate([total, sums[:4]], axis=0), ("shard", "ctx", "tp"))
    grad_embed = total[: seqs * shards].astype(BF)
    own_pre = lax.dynamic_slice_in_dim(time_pre, x * n2, n2, axis=1)
    grad_pre = jax.vjp(silu_fn, own_pre)[1](contract(grad_embed, w_time2, 1, 1))[0].astype(BF)
    grad_pre = jnp.swapaxes(shard_gather(grad_pre), 0, 1).reshape(seqs * shards, width)
    g_time1 = contract(own_feats, grad_pre, 0, 0)
    g_time2 = contract(own_hidden, grad_embed, 0, 0)
    share = width // shards
    affine_sums = lax.dynamic_slice_in_dim(total[seqs * shards :], x * share, share, axis=1)
    g_gains = jnp.stack([affine_sums[0], affine_sums[2]], axis=1)
    g_shifts = jnp.stack([affine_sums[1], affine_sums[3]], axis=1)

    if fast:
        piece_out, piece_down = piece_both[: cuts[1]], piece_both[cuts[1] :]
    else:
        grads = jnp.concatenate([g_out, g_in, g_down], axis=1)
        near = tp_shift(jnp.stack([grads[1], grads[3]]), 1)
        half0 = (grads[0].astype(F32) + near[0].astype(F32))
        half2 = (grads[2].astype(F32) + near[1].astype(F32)).astype(BF)
        whole = (half0 + tp_shift(half2, 2).astype(F32)).astype(BF)
        marks = (0, n_out, n_out + n_in, n_out + n_in + n_down)
        whole = jnp.concatenate([whole[marks[i] : marks[i + 1]].reshape(shards, -1, width) for i in range(3)], axis=1)
        piece = shard_scatter(whole).astype(BF)
        qkv_piece = shard_scatter(g_qkv.reshape(shards, width // shards, 3 * local)).astype(BF)
        piece = lax.psum(piece, "ctx").astype(F32)
        qkv_piece = lax.psum(qkv_piece, "ctx").astype(F32)
        piece_out, piece_in, piece_down = piece[: cuts[1]], piece[cuts[1] : cuts[2]], piece[cuts[2] :]
    return (
        result, grad_tokens.astype(F32), g_time1, g_time2, qkv_piece.reshape(w_qkv.shape),
        piece_out, piece_in, piece_down, g_gains, g_shifts,
    )


def solution(mesh):
    placed = (
        P("shard", "ctx", None), P("shard", "ctx"), P("shard"), P("shard", None), P("shard", None),
        P("shard", None, "tp"), P(("tp", "shard"), None), P("shard", "tp"), P(("tp", "shard"), None),
        P("shard", None), P("shard", None), P("shard", "ctx", None),
    )
    return jax.shard_map(
        body,
        mesh=mesh,
        in_specs=placed,
        out_specs=(
            P("shard", "ctx", None), P("shard", "ctx", None), P("shard", None), P("shard", None),
            P("shard", None, "tp"), P(("tp", "shard"), None), P("shard", "tp"), P(("tp", "shard"), None),
            P("shard", None), P("shard", None),
        ),
        check_vma=False,
    )
```
